512 devices in a mesh: ctx: 128 (over y_lo, x, z), head: 4 (over y_hi, core).
Axes of the slice: x: 4, y: 4 (y_hi: 2, y_lo: 2; y = y_hi * 2 + y_lo), z: 16, core: 2. Of those that a mesh axis runs over, the one named last changes fastest.
Arguments:
- hidden: bfloat16 [16384, 8192], P('ctx', 'head'), may hold values from -6 to 6
- frozen_query_rows: bfloat16 [16384, 3072], P('ctx', 'head'), may hold values from -101 to 101
- frozen_key_rows: bfloat16 [16384, 256], P('ctx'), may hold values from -5 to 5
- frozen_value_rows: bfloat16 [16384, 256], P('ctx'), may hold values from -6 to 6
- adapter_down_factors: bfloat16 [8192, 64], P('head'), may hold values from -0.0625 to 0.0625
- query_up_factor: bfloat16 [32, 3072], P(None, 'head'), may hold values from -1 to 1
- value_up_factor: bfloat16 [32, 256], replicated, may hold values from -1 to 1
- slot_span_order: int32 [256], replicated, may hold values from 0 to 255, each once
Outputs:
- attended: bfloat16 [16384, 3072], P('ctx', 'head')
- log_normalizer: float32 [24, 16384], P('head', 'ctx')
The draws below stay inside these ranges and needn't reach their ends.
Inputs may be any that keep to these rules, and one draw needn't show every extreme that they name: `slot_span_order`: every span number appears once.
All inputs are finite; a program needn't handle non-finite values.
Results may differ from the reference program's by a relative error of at most 0.018.
Values may be sent and summed in bfloat16 or wider, within the bound.
A program may use at most 64 MiB of HBM per device.

```python
import math
import jax
import jax.numpy as jnp
from jax import lax

MODEL_WIDTH = 8192
HEAD_SIZE = 128
QUERY_HEADS = 24
KEY_VALUE_HEADS = 2
ADAPTER_RANK = 32
CH = 64
SPANS = 256
TOKENS = 16384


def joint_fields(key):
    key_source = jax.random.fold_in(key, 17)
    query_source = jax.random.fold_in(key, 29)
    key_field = jnp.clip(jax.random.normal(key_source, (TOKENS, KEY_VALUE_HEADS * HEAD_SIZE), jnp.float32), -5.0, 5.0)
    query_field = jnp.clip(jax.random.normal(query_source, (TOKENS, QUERY_HEADS * HEAD_SIZE), jnp.float32), -5.0, 5.0)
    return (query_field, key_field)


def draw_frozen_query_rows(key, part):
    return joint_fields(key)[0].astype(jnp.bfloat16)


def draw_frozen_key_rows(key, part):
    return joint_fields(key)[1].astype(jnp.bfloat16)


def level_of(key, dims, pieces, least, high):
    gain = 1.0
    for dim, blocks in pieces:
        draws = jax.random.uniform(jax.random.fold_in(jax.random.fold_in(key, 6), dim), (blocks,), jnp.float32, least / len(pieces), high / len(pieces))
        gain = gain * jnp.repeat(jnp.exp(draws), dims[dim] // blocks).reshape((-1,) + (1,) * (len(dims) - 1 - dim))
    return gain


def gaussian(key, shape, width, bound, shards=(), kind=jnp.bfloat16):
    gain = level_of(key, shape, shards, -0.22, 0.18) if shards else 1.0
    values = jax.random.normal(key, shape, jnp.float32) * width * gain
    return jnp.minimum(jnp.maximum(values, -bound), bound).astype(kind)


def setup_inputs(seed: int = 0) -> dict:
    arg_keys = jax.random.split(jax.random.key(seed), 9)
    hidden = gaussian(arg_keys[0], (TOKENS, MODEL_WIDTH), 1.0, 6.0, ((0, 128), (1, 4)))
    frozen_query_rows = draw_frozen_query_rows(jax.random.fold_in(arg_keys[8], 71), 0)
    frozen_key_rows = draw_frozen_key_rows(jax.random.fold_in(arg_keys[8], 71), 0)
    frozen_value_rows = gaussian(arg_keys[3], (TOKENS, KEY_VALUE_HEADS * HEAD_SIZE), 1.0, 6.0, ((0, 128),))
    adapter_down_factors = gaussian(arg_keys[4], (MODEL_WIDTH, 2 * ADAPTER_RANK), MODEL_WIDTH ** -0.5, 0.0625, ((0, 4),))
    query_up_factor = gaussian(arg_keys[5], (ADAPTER_RANK, QUERY_HEADS * HEAD_SIZE), ADAPTER_RANK ** -0.5, 1.0, ((1, 4),))
    value_up_factor = gaussian(arg_keys[6], (ADAPTER_RANK, KEY_VALUE_HEADS * HEAD_SIZE), ADAPTER_RANK ** -0.5, 1.0)
    slot_span_order = jax.random.permutation(arg_keys[7], SPANS).astype(jnp.int32)
    return dict(hidden=hidden, frozen_query_rows=frozen_query_rows, frozen_key_rows=frozen_key_rows, frozen_value_rows=frozen_value_rows, adapter_down_factors=adapter_down_factors, query_up_factor=query_up_factor, value_up_factor=value_up_factor, slot_span_order=slot_span_order)


adapter_scale = 0.5

def spread_positions(span_ids, span_len):
    return (span_ids[:, None] * span_len + jnp.arange(span_len, dtype=jnp.int32)[None, :]).reshape(-1)

def reference(hidden, frozen_query_rows, frozen_key_rows, frozen_value_rows, adapter_down_factors, query_up_factor, value_up_factor, slot_span_order):
    adapter_bottleneck = jnp.dot(hidden, adapter_down_factors, preferred_element_type=jnp.float32).astype(jnp.bfloat16)
    query_matrix = (frozen_query_rows.astype(jnp.float32) + adapter_scale * jnp.dot(adapter_bottleneck[:, :ADAPTER_RANK], query_up_factor, preferred_element_type=jnp.float32)).astype(jnp.bfloat16)
    value_matrix = (frozen_value_rows.astype(jnp.float32) + adapter_scale * jnp.dot(adapter_bottleneck[:, ADAPTER_RANK:], value_up_factor, preferred_element_type=jnp.float32)).astype(jnp.bfloat16)
    position = spread_positions(slot_span_order.astype(jnp.int32), CH).astype(jnp.int32)
    group_size = QUERY_HEADS // KEY_VALUE_HEADS
    query_block = math.gcd(TOKENS, 512)
    block_count = TOKENS // query_block
    factor = 1.0 / math.sqrt(HEAD_SIZE)

    def one_tile(flat):
        flat = flat.astype(jnp.int32)
        zero_index = jnp.zeros((), jnp.int32)
        head_id = (flat // block_count).astype(jnp.int32)
        block_id = (flat % block_count).astype(jnp.int32)
        row_start = (block_id * query_block).astype(jnp.int32)
        head_column = (head_id * HEAD_SIZE).astype(jnp.int32)
        kv_column = (head_id // group_size * HEAD_SIZE).astype(jnp.int32)
        q_rows = lax.dynamic_slice(query_matrix, (row_start, head_column), (query_block, HEAD_SIZE)).astype(jnp.float32)
        k_rows = lax.dynamic_slice(frozen_key_rows, (zero_index, kv_column), (TOKENS, HEAD_SIZE)).astype(jnp.float32)
        v_rows = lax.dynamic_slice(value_matrix, (zero_index, kv_column), (TOKENS, HEAD_SIZE)).astype(jnp.float32)
        q_pos = lax.dynamic_slice(position, (row_start,), (query_block,))
        scores = lax.dot_general(q_rows, k_rows, (((1,), (1,)), ((), ())), precision=lax.Precision.HIGHEST) * factor
        visible = position[None, :] <= q_pos[:, None]
        row_max = lax.optimization_barrier(jnp.max(jnp.where(visible, scores, -jnp.inf), axis=1))
        weights = jnp.where(visible, jnp.exp(scores - row_max[:, None]), 0.0)
        denominator = lax.optimization_barrier(jnp.sum(weights, axis=1))
        rounded = lax.optimization_barrier(weights.astype(jnp.bfloat16)).astype(jnp.float32)
        numerator = jnp.dot(rounded, v_rows, precision=lax.Precision.HIGHEST)
        result = (numerator / denominator[:, None]).astype(jnp.bfloat16)
        return (result, row_max + jnp.log(denominator))
    tiles, normals = lax.map(one_tile, jnp.arange(QUERY_HEADS * block_count, dtype=jnp.int32))
    attended = tiles.reshape(QUERY_HEADS, TOKENS, HEAD_SIZE).transpose(1, 0, 2).reshape(TOKENS, QUERY_HEADS * HEAD_SIZE)
    return (attended, normals.reshape(QUERY_HEADS, TOKENS))
```

```python
import functools
import math

import jax
import jax.numpy as jnp
from jax import lax
from jax.experimental import pallas as pl
from jax.experimental.pallas import tpu as pltpu
from jax.sharding import PartitionSpec as P

HEAD_SIZE = 128
ADAPTER_RANK = 32
SPAN = 64
NX, NZ = 4, 16
GROUP = NZ * SPAN
GROUPS = 8
HEADS_DEV = 6
ROWS = HEADS_DEV * 128
LAG = 5
LOG2_SCALE = math.log2(math.e) / math.sqrt(HEAD_SIZE)
LN2 = math.log(2.0)
MASKED = -1e30
MESH = pl.DeviceIdType.MESH

OFFSETS = (0, 3, -3, 6, -6, 8, 1, 4, -2, 7, -5, -1, 2, -4, 5, -7)
PARTS = ((0, 192), (192, 192), (384, 320), (704, 320))
HALVES = ((0, 384), (384, 640))
ORDER = ((0, 0), (0, 1), (1, 0), (3, 0), (1, 1), (3, 1), (2, 0), (2, 1))
BASE = {which: i * GROUP for i, which in enumerate(ORDER)}
COPIES = 29
SHARED = (0, 1, 3, 2)


def body(
    hidden_hbm, fq_hbm, fk_hbm, fv_hbm, down_hbm, qup_hbm, vup_hbm, order_ref,
    out_ref, lse_ref,
    hidden_v, fq_v, fv_v, down_v, qup_v, vup_v,
    low_own, low_recv, vtmp,
    q_own, q_other, kbuf, vbuf, bias, tri,
    s0, s1, x0, x1, maxima, l_s, acc, weights,
    num_send, num_recv, stat_send, stat_recv,
    load_sem, low_ssem, low_rsem, ssem, rsem, q_sem, f_ssem, f_rsem,
):
    ctx = lax.axis_index("ctx")
    head = lax.axis_index("head")
    core = lax.rem(head, 2)
    kv = head // 2
    z = lax.rem(ctx, NZ)
    x = lax.rem(ctx // NZ, NX)
    y = ctx // (NZ * NX)

    def at(yy, xx, zz):
        return {"ctx": yy * (NX * NZ) + xx * NZ + zz, "head": head}

    def along_z(step):
        return at(y, x, lax.rem(z + step + NZ, NZ))

    y_peer = at(1 - y, x, z)
    x_nb = (at(y, lax.rem(x + 1, NX), z), at(y, lax.rem(x + NX - 1, NX), z))
    other_core = 2 * kv + (1 - core)
    far_same = 2 * (1 - kv) + core
    far_other = 2 * (1 - kv) + (1 - core)
    head_peers = tuple({"ctx": ctx, "head": h} for h in (other_core, far_same, far_other))
    sibling = head_peers[0]
    z_peers = tuple(along_z(d) for d in (3, -3, 6, -6, 8, 1, -1))

    barrier = pltpu.get_barrier_semaphore()
    for peer in (*z_peers, *head_peers, y_peer, *x_nb):
        pl.semaphore_signal(barrier, inc=1, device_id=peer, device_id_type=MESH)

    row0 = pl.multiple_of(core * SPAN, SPAN)
    col0 = pl.multiple_of(kv * HEAD_SIZE, 128)
    col = pl.ds(col0, HEAD_SIZE)
    loads = [
        pltpu.make_async_copy(fk_hbm.at[pl.ds(row0, SPAN), col], kbuf.at[pl.ds(0, SPAN), :], load_sem.at[0]),
        pltpu.make_async_copy(hidden_hbm, hidden_v, load_sem.at[1]),
        pltpu.make_async_copy(down_hbm, down_v, load_sem.at[2]),
        pltpu.make_async_copy(fv_hbm.at[:, col], fv_v, load_sem.at[3]),
        pltpu.make_async_copy(vup_hbm.at[:, col], vup_v, load_sem.at[4]),
        pltpu.make_async_copy(fq_hbm, fq_v, load_sem.at[5]),
        pltpu.make_async_copy(qup_hbm, qup_v, load_sem.at[6]),
    ]
    for load in loads:
        load.start()

    bufs = (kbuf, vbuf)
    own = BASE[0, 0]
    plan = []
    for i, there in enumerate((128, 64, 256, 192, 320)):
        plan.append((own, own + there, SPAN, z_peers[i]))
    for first, rows, ups in ((0, 192, (704, 384)), (192, 128, (896, 576))):
        for way in range(2):
            plan.append((own + first, own + ups[way], rows, z_peers[5 + way]))
    for first, rows in PARTS:
        for way in range(2):
            plan.append((own + first, BASE[3 - 2 * way, 0] + first, rows, x_nb[way]))
    for i, (first, rows) in enumerate(PARTS):
        way = i % 2
        plan.append((BASE[3 - 2 * way, 0] + first, BASE[2, 0] + first, rows, x_nb[way]))
    for dx in SHARED:
        for first, rows in HALVES:
            plan.append((BASE[dx, 0] + first, BASE[dx, 1] + first, rows, sibling))

    def copy(t, i):
        src, dst, rows, device = plan[i]
        return pltpu.make_async_remote_copy(
            src_ref=bufs[t].at[pl.ds(src, rows), :],
            dst_ref=bufs[t].at[pl.ds(dst, rows), :],
            send_sem=ssem.at[t * COPIES + i],
            recv_sem=rsem.at[t * COPIES + i],
            device_id=device,
            device_id_type=MESH,
        )

    events = (
        ((), (0, 1, 2, 3, 4)),
        ((0, 1), (5, 6, 9, 10)),
        ((2, 3, 4), (7, 8, 11, 12, 21)),
        ((5, 6, 7, 8), (13, 14, 15, 16, 22)),
        ((9, 10, 11, 12), (17, 18, 23, 25)),
        ((13, 14, 15, 16), (19, 20, 24, 26)),
        ((17, 18), (27,)),
        ((19, 20), (28,)),
    )

    def event(t, e):
        for i in events[e][0]:
            copy(t, i).wait_recv()
        for i in events[e][1]:
            copy(t, i).start()

    def shared(t, j):
        copy(t, 21 + 2 * j).wait_recv()
        copy(t, 22 + 2 * j).wait_recv()

    K, V = 0, 1
    pl.semaphore_wait(barrier, 13)
    loads[0].wait()
    event(K, 0)

    loads[1].wait()
    loads[2].wait()
    partial = lax.dot_general(
        hidden_v[...], down_v[...], (((1,), (1,)), ((), ())), preferred_element_type=jnp.float32
    )
    low_own[...] = jnp.concatenate([partial[:64], partial[64:]], axis=1)

    def low_copy(k):
        return pltpu.make_async_remote_copy(
            src_ref=low_own, dst_ref=low_recv.at[k], send_sem=low_ssem.at[k], recv_sem=low_rsem.at[k],
            device_id=head_peers[k], device_id_type=MESH,
        )

    column = lax.broadcasted_iota(jnp.int32, (SPAN, GROUP), 1)
    token = lax.broadcasted_iota(jnp.int32, (SPAN, GROUP), 0)
    tri[...] = jnp.where((column < SPAN) & (column > token), MASKED, 0.0)
    l_s[...] = jnp.zeros_like(l_s)
    for k in (1, 2, 0):
        low_copy(k).start()

    sublane = lax.broadcasted_iota(jnp.int32, (8, GROUP), 0)
    lane_span = lax.broadcasted_iota(jnp.int32, (8, GROUP), 1) // SPAN
    limit = jnp.zeros((8, GROUP), jnp.int32)
    for tile, yy in enumerate((1 - y, y)):
        for a in range(2):
            mine = order_ref[2 * (yy * (NX * NZ) + x * NZ + z) + a]
            limit = jnp.where(sublane == 2 * tile + a, mine, limit)
    for g, (dx, other) in enumerate(ORDER):
        found = jnp.zeros((8, GROUP), jnp.int32)
        chip = y * (NX * NZ) + lax.rem(x + dx, NX) * NZ
        slot = 1 - core if other else core
        for i, dz in enumerate(OFFSETS):
            span = order_ref[2 * (chip + lax.rem(z + dz + NZ, NZ)) + slot]
            found = jnp.where(lane_span == i, span, found)
        bias[g] = jnp.where(found <= limit, 0.0, MASKED)

    loads[3].wait()
    loads[4].wait()
    for k in (0, 1, 2):
        low_copy(k).wait_recv()
    packed = (low_own[...] + low_recv[0]) + (low_recv[1] + low_recv[2])
    low = jnp.concatenate([packed[:, :64], packed[:, 64:]], axis=0).astype(jnp.bfloat16)
    update = jnp.dot(low[:, ADAPTER_RANK:], vup_v[...], preferred_element_type=jnp.float32)
    vtmp[...] = (fv_v[...].astype(jnp.float32) + 0.5 * update).astype(jnp.bfloat16)
    vbuf[pl.ds(0, SPAN), :] = vtmp[pl.ds(row0, SPAN), :]

    loads[5].wait()
    loads[6].wait()
    q_update = jnp.dot(low[:, :ADAPTER_RANK], qup_v[...], preferred_element_type=jnp.float32)
    queries = (fq_v[...].astype(jnp.float32) + 0.5 * q_update).astype(jnp.bfloat16)
    event(V, 0)
    for h in range(HEADS_DEV):
        q_own[pl.ds(h * 128, 128), :] = queries[:, h * 128 : (h + 1) * 128]
    event(K, 1)
    q_copy = pltpu.make_async_remote_copy(
        src_ref=q_own, dst_ref=q_other, send_sem=q_sem.at[0], recv_sem=q_sem.at[1],
        device_id=y_peer, device_id_type=MESH,
    )
    q_copy.start()
    event(K, 2)
    event(K, 4)
    event(K, 3)

    qs = (q_other, q_own)
    sbuf, xbuf = (s0, s1), (x0, x1)

    def first_row(g):
        return g * GROUP if isinstance(g, int) else pl.multiple_of(g * GROUP, GROUP)

    def score(g, tile, buf, diagonal=None):
        s = lax.dot_general(
            qs[tile][...], kbuf[pl.ds(first_row(g), GROUP), :], (((1,), (1,)), ((), ())),
            preferred_element_type=jnp.float32,
        )
        for c in range(2 * HEADS_DEV):
            a = c % 2
            rows = slice(c * SPAN, (c + 1) * SPAN)
            add = bias[g, 2 * tile + a : 2 * tile + a + 1, :]
            if diagonal is not None:
                add = add + jnp.where(diagonal == a, 1.0, 0.0) * tri[...]
            part = s[rows] * LOG2_SCALE + add
            sbuf[buf][rows, :] = part
            xbuf[buf][rows, :] = functools.reduce(
                jnp.maximum, [part[:, i * 128 : (i + 1) * 128] for i in range(GROUP // 128)]
            )

    def weigh(g, tile, buf):
        rows = pl.ds(tile * ROWS, ROWS)
        new = jnp.broadcast_to(jnp.max(xbuf[buf][...], axis=1, keepdims=True), (ROWS, 128))
        static = isinstance(g, int) and g == 0
        if not static:
            old = maxima[g - 1, rows, :]
            new = jnp.maximum(old, new)
        maxima[g, rows, :] = new
        p = jnp.exp2(sbuf[buf][...] - new[:, :1])
        total = functools.reduce(jnp.add, [p[:, i * 128 : (i + 1) * 128] for i in range(GROUP // 128)])
        if static:
            l_s[rows, :] = total
        else:
            l_s[rows, :] = l_s[rows, :] * jnp.exp2(old - new) + total
        weights[g, rows, :] = p.astype(jnp.bfloat16)

    def apply(g, tile):
        rows = pl.ds(tile * ROWS, ROWS)
        pv = jnp.dot(weights[g, rows, :], vbuf[pl.ds(first_row(g), GROUP), :], preferred_element_type=jnp.float32)
        if isinstance(g, int) and g == 0:
            acc[rows, :] = pv
        else:
            acc[rows, :] = acc[rows, :] * jnp.exp2(maxima[g - 1, rows, :] - maxima[g, rows, :]) + pv

    score(0, 1, 0, diagonal=core)
    shared(K, 0)
    score(1, 1, 1, diagonal=1 - core)
    weigh(0, 1, 0)
    event(V, 1)
    q_copy.wait_recv()
    score(0, 0, 0)
    weigh(1, 1, 1)
    event(K, 6)
    score(1, 0, 1)
    weigh(0, 0, 0)
    event(V, 2)
    event(K, 5)

    def on(g, table):
        for at_g, run in table:
            pl.when(g == at_g)(run)

    def early(g, _):
        on(g, ((4, lambda: shared(K, 1)),))
        score(g, 1, 0)
        weigh(g - 1, 0, 1)
        on(g, ((3, lambda: event(V, 4)), (4, lambda: event(V, 3))))
        score(g, 0, 1)
        weigh(g, 1, 0)
        return 0

    lax.fori_loop(2, LAG, early, 0)
    event(K, 7)

    shared(K, 2)
    score(LAG, 1, 0)
    weigh(LAG - 1, 0, 1)
    apply(0, 0)
    event(V, 6)
    score(LAG, 0, 1)
    weigh(LAG, 1, 0)
    apply(0, 1)

    def late(g, _):
        on(g, ((6, lambda: shared(V, 0)), (7, lambda: shared(K, 3)), (7, lambda: event(V, 5))))
        score(g, 1, 0)
        weigh(g - 1, 0, 1)
        apply(g - LAG, 0)
        score(g, 0, 1)
        weigh(g, 1, 0)
        apply(g - LAG, 1)
        return 0

    lax.fori_loop(LAG + 1, GROUPS, late, 0)
    weigh(7, 0, 1)
    apply(3, 0)
    apply(3, 1)

    def rest(g, _):
        on(g, ((4, lambda: shared(V, 1)), (5, lambda: shared(V, 2)), (5, lambda: event(V, 7))))
        apply(g, 0)
        apply(g, 1)
        return 0

    lax.fori_loop(4, 7, rest, 0)
    shared(V, 3)
    apply(7, 0)

    for h in range(HEADS_DEV):
        rows = pl.ds(h * 128, 128)
        num_send[rows, :] = acc[rows, :].astype(jnp.bfloat16)
        stat_send[pl.ds(h, 1), :] = maxima[7, rows, :].T[0:1, :]
        stat_send[pl.ds(8 + h, 1), :] = jnp.sum(l_s[rows, :].T, axis=0, keepdims=True)
    backs = [
        pltpu.make_async_remote_copy(
            src_ref=src, dst_ref=dst, send_sem=f_ssem.at[i], recv_sem=f_rsem.at[i], device_id=y_peer, device_id_type=MESH
        )
        for i, (src, dst) in enumerate(((num_send, num_recv), (stat_send, stat_recv)))
    ]
    for back in backs:
        back.start()
    apply(7, 1)
    for t in range(2):
        for i in range(COPIES):
            copy(t, i).wait_send()
    for k in range(3):
        low_copy(k).wait_send()
    q_copy.wait_send()
    for back in backs:
        back.wait_recv()
    for h in range(HEADS_DEV):
        rows = pl.ds(ROWS + h * 128, 128)
        part = pl.ds(h * 128, 128)
        other_max = jnp.broadcast_to(stat_recv[pl.ds(h, 1), :], (128, 128)).T
        other_total = jnp.broadcast_to(stat_recv[pl.ds(8 + h, 1), :], (128, 128)).T
        own_max = maxima[7, rows, :]
        new = jnp.maximum(own_max, other_max)
        own_scale = jnp.exp2(own_max - new)
        other_scale = jnp.exp2(other_max - new)
        total = jnp.sum(l_s[rows, :], axis=1, keepdims=True) * own_scale + other_total * other_scale
        number = acc[rows, :] * own_scale + num_recv[part, :].astype(jnp.float32) * other_scale
        out_ref[:, h * 128 : (h + 1) * 128] = (number / total).astype(jnp.bfloat16)
        lse_ref[pl.ds(h, 1), :] = (new * LN2 + jnp.log(total)).T[0:1, :]
    for back in backs:
        back.wait_send()


def local(hidden, fq, fk, fv, down, qup, vup, order):
    bf16, f32 = jnp.bfloat16, jnp.float32
    hbm = pl.BlockSpec(memory_space=pl.ANY)
    vmem = pl.BlockSpec(memory_space=pltpu.VMEM)
    dma = pltpu.SemaphoreType.DMA
    keys = GROUPS * GROUP
    return pl.pallas_call(
        body,
        name="shared_attention",
        out_shape=(
            jax.ShapeDtypeStruct((128, ROWS), bf16),
            jax.ShapeDtypeStruct((HEADS_DEV, 128), f32),
        ),
        in_specs=[hbm] * 7 + [pl.BlockSpec(memory_space=pltpu.SMEM)],
        out_specs=[vmem, vmem],
        scratch_shapes=[
            pltpu.VMEM((128, 2048), bf16),
            pltpu.VMEM((128, ROWS), bf16),
            pltpu.VMEM((128, 128), bf16),
            pltpu.VMEM((64, 2048), bf16),
            pltpu.VMEM((32, ROWS), bf16),
            pltpu.VMEM((32, 128), bf16),
            pltpu.VMEM((64, 128), f32),
            pltpu.VMEM((3, 64, 128), f32),
            pltpu.VMEM((128, 128), bf16),
            pltpu.VMEM((ROWS, 128), bf16),
            pltpu.VMEM((ROWS, 128), bf16),
            pltpu.VMEM((keys, 128), bf16),
            pltpu.VMEM((keys, 128), bf16),
            pltpu.VMEM((GROUPS, 8, GROUP), f32),
            pltpu.VMEM((SPAN, GROUP), f32),
            pltpu.VMEM((ROWS, GROUP), f32),
            pltpu.VMEM((ROWS, GROUP), f32),
            pltpu.VMEM((ROWS, 128), f32),
            pltpu.VMEM((ROWS, 128), f32),
            pltpu.VMEM((GROUPS, 2 * ROWS, 128), f32),
            pltpu.VMEM((2 * ROWS, 128), f32),
            pltpu.VMEM((2 * ROWS, 128), f32),
            pltpu.VMEM((GROUPS, 2 * ROWS, GROUP), bf16),
            pltpu.VMEM((ROWS, 128), bf16),
            pltpu.VMEM((ROWS, 128), bf16),
            pltpu.VMEM((16, 128), f32),
            pltpu.VMEM((16, 128), f32),
            dma((7,)),
            dma((3,)),
            dma((3,)),
            dma((2 * COPIES,)),
            dma((2 * COPIES,)),
            dma((2,)),
            dma((2,)),
            dma((2,)),
        ],
        compiler_params=pltpu.CompilerParams(
            collective_id=0, has_side_effects=True, vmem_limit_bytes=60 * 2**20
        ),
    )(hidden, fq, fk, fv, down.T, qup, vup, order)


def solution(mesh):
    placed = (
        P("ctx", "head"),
        P("ctx", "head"),
        P("ctx", None),
        P("ctx", None),
        P("head", None),
        P(None, "head"),
        P(),
        P(),
    )
    return jax.shard_map(
        local,
        mesh=mesh,
        in_specs=placed,
        out_specs=(P("ctx", "head"), P("head", "ctx")),
        check_vma=False,
    )
```
